32 devices in a mesh: dp: 2 (over core), seq: 16 (over z, y, x).
Axes of the slice: x: 2, y: 2, z: 4, core: 2. Of those that a mesh axis runs over, the one named last changes fastest.
Arguments:
- hidden_in: bfloat16 [4, 4096, 768], P('dp', 'seq'), may hold values from -6 to 6
- cotangent: bfloat16 [4, 4096, 768], P('dp', 'seq'), may hold values from -6 to 6
- segments: int32 [4, 4096], P('dp'), may hold values from 0 to 20, as said below
- pad_mask: int32 [4, 4096], P('dp'), may hold values 0 or 1
- w_qkv: bfloat16 [768, 2304], P(('dp', 'seq')), may hold values from -0.21875 to 0.21875
- b_query: bfloat16 [768], P(('dp', 'seq')), may hold values from -3 to 3
- b_value: bfloat16 [768], P(('dp', 'seq')), may hold values from -3 to 3
- w_out: bfloat16 [768, 768], P(('dp', 'seq')), may hold values from -0.875 to 0.875
- b_out: bfloat16 [768], P(('dp', 'seq')), may hold values from -3 to 3
- norm1_gain: bfloat16 [768], P(('dp', 'seq')), may hold values from 0.099609375 to 1.8984375
- norm1_bias: bfloat16 [768], P(('dp', 'seq')), may hold values from -3 to 3
- w_up: bfloat16 [768, 3072], P(('dp', 'seq')), may hold values from -0.21875 to 0.21875
- b_up: bfloat16 [3072], P(('dp', 'seq')), may hold values from -3 to 3
- w_down: bfloat16 [3072, 768], P(('dp', 'seq')), may hold values from -0.109375 to 0.109375
- b_down: bfloat16 [768], P(('dp', 'seq')), may hold values from -3 to 3
- norm2_gain: bfloat16 [768], P(('dp', 'seq')), may hold values from 0.099609375 to 1.8984375
- norm2_bias: bfloat16 [768], P(('dp', 'seq')), may hold values from -3 to 3
Outputs:
- hidden_out: bfloat16 [4, 4096, 768], P('dp', 'seq')
- hidden_grad: float32 [4, 4096, 768], P('dp', 'seq')
- grad_w_qkv: float32 [768, 2304], P(('dp', 'seq'))
- grad_b_query: float32 [768], P(('dp', 'seq'))
- grad_b_value: float32 [768], P(('dp', 'seq'))
- grad_w_out: float32 [768, 768], P(('dp', 'seq'))
- grad_b_out: float32 [768], P(('dp', 'seq'))
- grad_norm1_gain: float32 [768], P(('dp', 'seq'))
- grad_norm1_bias: float32 [768], P(('dp', 'seq'))
- grad_w_up: float32 [768, 3072], P(('dp', 'seq'))
- grad_b_up: float32 [3072], P(('dp', 'seq'))
- grad_w_down: float32 [3072, 768], P(('dp', 'seq'))
- grad_b_down: float32 [768], P(('dp', 'seq'))
- grad_norm2_gain: float32 [768], P(('dp', 'seq'))
- grad_norm2_bias: float32 [768], P(('dp', 'seq'))
The draws below stay inside these ranges and needn't reach their ends.
Inputs may be any that keep to these rules, and one draw needn't show every extreme that they name: `segments`: along a sequence the numbers never fall and change exactly where a document ends; the documents before the last carry 0, 1, 2 and so on, and the last document of every sequence carries 21 - 1; every document has 200 to 768 tokens except the last of a sequence, which may be cut short; one of the first two documents of every sequence has exactly 768 tokens.
All inputs are finite; a program needn't handle non-finite values. No bound on the sum of `pad_mask` on one device may be relied on, other than what follows from the above.
Results may differ from the reference program's by a relative error of at most 0.015.
Values may be sent and summed in bfloat16 or wider, within the bound.
A program may use at most 320 MiB of HBM per device.

```python
import jax
import jax.numpy as jnp
from jax import lax

D = 768
HEADS = 12
HEAD = 64
FF = 3072
TPD = 256
DOC_MAX = 768
MIN_DOC = 200
REACH = 3
SEQS = 4
SEQ_LEN = 4096


def draw_segments(key, part):
    count = SEQ_LEN // MIN_DOC + 1

    def one_row(row_key):
        len_key, place_key = jax.random.split(row_key)
        lengths = jax.random.randint(len_key, (count,), MIN_DOC, DOC_MAX + 1)
        place = jax.random.randint(place_key, (), 0, 2)
        lengths = jnp.where(jnp.arange(count) == place, DOC_MAX, lengths)
        ends = jnp.cumsum(lengths)
        position = jnp.arange(SEQ_LEN)
        numbers = jnp.sum((ends[None, :] <= position[:, None]).astype(jnp.int32), axis=1).astype(jnp.int32)
        last_number = numbers[SEQ_LEN - 1]
        return jnp.where(numbers == last_number, count - 1, numbers).astype(jnp.int32)
    return jax.vmap(one_row)(jax.random.split(jax.random.fold_in(key, 11), SEQS))


def place_ends(drawn, rng, least, high):
    shape = drawn.shape
    index_at = [jax.random.randint(jax.random.fold_in(rng, axis), (), 0, shape[axis]) for axis in range(len(shape))]
    drawn = drawn.at[tuple(index_at)].set(least)
    longest = shape.index(max(shape))
    index_at[longest] = (index_at[longest] + 1) % shape[longest]
    return drawn.at[tuple(index_at)].set(high)


def block_levels(key, shape, shards, smallest, largest):
    level = 1.0
    for dim, shards_of in shards:
        draws = jax.random.uniform(jax.random.fold_in(jax.random.fold_in(key, 6), dim), (shards_of,), jnp.float32, smallest / len(shards), largest / len(shards))
        level = level * jnp.repeat(jnp.exp(draws), shape[dim] // shards_of).reshape((-1,) + (1,) * (len(shape) - 1 - dim))
    return level


def scatter_about(stream_key, shape, deviation, bound, pieces=(), kind=jnp.bfloat16):
    level = block_levels(stream_key, shape, pieces, -0.22, 0.18) if pieces else 1.0
    entries = jax.random.normal(stream_key, shape, jnp.float32) * deviation * level
    return jnp.minimum(jnp.maximum(entries, -bound), bound).astype(kind)


def setup_inputs(seed: int = 0) -> dict:
    arg_keys = jax.random.split(jax.random.key(seed), 18)
    hidden_in = scatter_about(arg_keys[0], (SEQS, SEQ_LEN, D), 1.0, 6.0, ((0, 2), (1, 16)))
    cotangent = scatter_about(arg_keys[1], (SEQS, SEQ_LEN, D), 1.0, 6.0, ((0, 2), (1, 16)))
    segments = draw_segments(jax.random.fold_in(arg_keys[17], 71), 0)
    pad_mask = place_ends((jax.random.randint(arg_keys[3], (SEQS, SEQ_LEN), 0, 8) < 7).astype(jnp.int32), jax.random.fold_in(arg_keys[3], 1), 0, 1)
    w_qkv = scatter_about(arg_keys[4], (D, 3 * D), D ** -0.5, 0.21875, ((0, 32),))
    b_query = scatter_about(arg_keys[5], (D,), 0.5, 3.0, ((0, 32),))
    b_value = scatter_about(arg_keys[6], (D,), 0.5, 3.0, ((0, 32),))
    w_out = scatter_about(arg_keys[7], (D, D), (D // 16) ** -0.5, 0.875, ((0, 32),))
    b_out = scatter_about(arg_keys[8], (D,), 0.5, 3.0, ((0, 32),))
    norm1_gain = jnp.clip(1.0 + 0.18 * jax.random.normal(arg_keys[9], (D,), jnp.float32), 0.099609375, 1.8984375).astype(jnp.bfloat16)
    norm1_bias = scatter_about(arg_keys[10], (D,), 0.5, 3.0, ((0, 32),))
    w_up = scatter_about(arg_keys[11], (D, FF), D ** -0.5, 0.21875, ((0, 32),))
    b_up = scatter_about(arg_keys[12], (FF,), 0.5, 3.0, ((0, 32),))
    w_down = scatter_about(arg_keys[13], (FF, D), FF ** -0.5, 0.109375, ((0, 32),))
    b_down = scatter_about(arg_keys[14], (D,), 0.5, 3.0, ((0, 32),))
    norm2_gain = jnp.clip(1.0 + 0.18 * jax.random.normal(arg_keys[15], (D,), jnp.float32), 0.099609375, 1.8984375).astype(jnp.bfloat16)
    norm2_bias = scatter_about(arg_keys[16], (D,), 0.5, 3.0, ((0, 32),))
    return {"hidden_in": hidden_in, "cotangent": cotangent, "segments": segments, "pad_mask": pad_mask, "w_qkv": w_qkv, "b_query": b_query, "b_value": b_value, "w_out": w_out, "b_out": b_out, "norm1_gain": norm1_gain, "norm1_bias": norm1_bias, "w_up": w_up, "b_up": b_up, "w_down": w_down, "b_down": b_down, "norm2_gain": norm2_gain, "norm2_bias": norm2_bias}


@jax.custom_vjp
def low(v):
    return lax.optimization_barrier(v.astype(jnp.bfloat16)).astype(jnp.float32)

@jax.custom_vjp
def low_back(v):
    return v

def low_keep(v):
    return (low(v), None)

def low_pass(kept, grad):
    return (grad,)

def back_keep(v):
    return (v, None)

def back_low(kept, grad):
    return (low(grad),)
low.defvjp(low_keep, low_pass)
low_back.defvjp(back_keep, back_low)

def normalize(resid, gain, shift):
    center = resid - lax.optimization_barrier(jnp.mean(resid, axis=-1, keepdims=True))
    spread = lax.optimization_barrier(jnp.mean(center * center, axis=-1, keepdims=True))
    return center * lax.rsqrt(spread + 1e-12) * gain + shift

def layer(state, seg_row, pad_row, params):
    mat_qkv, bias_query, bias_value, mat_out, bias_out, gain_one, shift_one, mat_up, bias_up, mat_down, bias_down, gain_two, shift_two = params
    length = state.shape[0]
    margin = REACH * TPD
    window = (2 * REACH + 1) * TPD
    state_low = low(state)
    bias_all = jnp.concatenate([bias_query, jnp.zeros_like(bias_query), bias_value])
    projected = low(low_back(jnp.dot(state_low, mat_qkv, precision=lax.Precision.HIGHEST) + bias_all))
    queries = projected[:, :D].reshape(length, HEADS, HEAD)
    keys_pad = jnp.pad(projected[:, D:2 * D], ((margin, margin), (0, 0))).reshape(length + 2 * margin, HEADS, HEAD)
    values_pad = jnp.pad(projected[:, 2 * D:], ((margin, margin), (0, 0))).reshape(length + 2 * margin, HEADS, HEAD)
    seg_pad = jnp.pad(seg_row, (margin, margin), constant_values=-1)
    mask_pad = jnp.pad(pad_row, (margin, margin))
    itself = jnp.arange(TPD)[:, None] + margin == jnp.arange(window)[None, :]

    def block(index):
        start = (index * TPD).astype(jnp.int32)
        query_blk = lax.dynamic_slice_in_dim(queries, start, TPD, 0)
        key_blk = lax.dynamic_slice_in_dim(keys_pad, start, window, 0)
        value_blk = lax.dynamic_slice_in_dim(values_pad, start, window, 0)
        seg_query = lax.dynamic_slice_in_dim(seg_row, start, TPD, 0)
        seg_keys = lax.dynamic_slice_in_dim(seg_pad, start, window, 0)
        mask_keys = lax.dynamic_slice_in_dim(mask_pad, start, window, 0)
        allowed = (seg_query[:, None] == seg_keys[None, :]) & ((mask_keys[None, :] == 1) | itself)
        scores = jnp.einsum('qhd,khd->hqk', query_blk, key_blk, precision=lax.Precision.HIGHEST) * 0.125
        scores = low_back(scores)
        scores = jnp.where(allowed[None], scores, -1e+30)
        top = lax.optimization_barrier(jnp.max(scores, axis=-1, keepdims=True))
        expo = jnp.exp(scores - top)
        probs = low(expo / lax.optimization_barrier(jnp.sum(expo, axis=-1, keepdims=True)))
        context = jnp.einsum('hqk,khd->qhd', probs, value_blk, precision=lax.Precision.HIGHEST)
        return context.reshape(TPD, D)
    context = lax.map(jax.checkpoint(block), jnp.arange(length // TPD, dtype=jnp.int32))
    context = low(low_back(context.reshape(length, D)))
    attn = low_back(jnp.dot(context, mat_out, precision=lax.Precision.HIGHEST) + bias_out)
    hidden = normalize(state + attn, gain_one, shift_one)
    up_pre = low_back(jnp.dot(low(hidden), mat_up, precision=lax.Precision.HIGHEST) + bias_up)
    active = low(jax.nn.gelu(up_pre, approximate=False))
    ffn = low_back(jnp.dot(active, mat_down, precision=lax.Precision.HIGHEST) + bias_down)
    return normalize(hidden + ffn, gain_two, shift_two)

def reference(hidden_in, cotangent, segments, pad_mask, w_qkv, b_query, b_value, w_out, b_out, norm1_gain, norm1_bias, w_up, b_up, w_down, b_down, norm2_gain, norm2_bias):
    params = (w_qkv.astype(jnp.float32), b_query.astype(jnp.float32), b_value.astype(jnp.float32), w_out.astype(jnp.float32), b_out.astype(jnp.float32), norm1_gain.astype(jnp.float32), norm1_bias.astype(jnp.float32), w_up.astype(jnp.float32), b_up.astype(jnp.float32), w_down.astype(jnp.float32), b_down.astype(jnp.float32), norm2_gain.astype(jnp.float32), norm2_bias.astype(jnp.float32))
    totals = tuple((jnp.zeros_like(param) for param in params))

    def one_sequence(carry, item):
        seq_in, seq_cot, seg_row, pad_row = item

        def forward(state, weights):
            return layer(layer(state, seg_row, pad_row, weights), seg_row, pad_row, weights)
        result, backward = jax.vjp(forward, seq_in.astype(jnp.float32), params)
        grad_out = seq_cot.astype(jnp.float32) * pad_row.astype(jnp.float32)[:, None]
        grad_in, grad_params = backward(grad_out)
        carry = jax.tree.map(lambda left, right: left + right, carry, grad_params)
        return (carry, (result.astype(jnp.bfloat16), grad_in))
    grads, (outputs, input_grads) = lax.scan(one_sequence, totals, (hidden_in, cotangent, segments, pad_mask))
    return (outputs, input_grads, grads[0], grads[1], grads[2], grads[3], grads[4], grads[5], grads[6], grads[7], grads[8], grads[9], grads[10], grads[11], grads[12])
```

```python
import functools

import jax
import jax.numpy as jnp
from jax import lax
from jax.experimental import pallas as pl
from jax.experimental.pallas import tpu as pltpu
from jax.sharding import PartitionSpec as P

HEADS = 12
HEAD = 64
PAIR = 2 * HEAD
REACH = 3
TILE = 256
LINE = 4

F32 = jnp.float32
BF16 = jnp.bfloat16


def pick_lanes(block, half):
    lanes = lax.broadcasted_iota(jnp.int32, block.shape, 1)
    keep = (lanes < HEAD) if half == 0 else (lanes >= HEAD)
    return jnp.where(keep, block, jnp.zeros_like(block))


def dot_nt(left, right):
    return lax.dot_general(left, right, (((1,), (1,)), ((), ())), preferred_element_type=F32)


def dot_tn(left, right):
    return lax.dot_general(left, right, (((0,), (0,)), ((), ())), preferred_element_type=F32)


def dot_nn(left, right):
    return lax.dot_general(left, right, (((1,), (0,)), ((), ())), preferred_element_type=F32)


def attend_kernel(span, q_ref, k_ref, v_ref, segq, segk, padk, ctx_ref, lse_ref, bias, scores):
    pair = pl.program_id(0)
    rows = q_ref.shape[0]
    window = k_ref.shape[0]
    tiles = rows // TILE
    for tile in range(tiles):
        at = slice(tile * TILE, (tile + 1) * TILE)
        low, high = span[tile, 0], span[tile, 1]

        @pl.when(pair == 0)
        def _():
            def fill(block, carry):
                cols = pl.ds(pl.multiple_of(block * TILE, TILE), TILE)
                row_at = lax.broadcasted_iota(jnp.int32, (TILE, TILE), 0) + (REACH * TILE + tile * TILE)
                col_at = lax.broadcasted_iota(jnp.int32, (TILE, TILE), 1) + block * TILE
                same = segq[at, :] == segk[:, cols]
                open_key = (padk[:, cols] == 1) | (row_at == col_at)
                bias[at, cols] = jnp.where(same & open_key, 0.0, -1e30)
                return carry
            lax.fori_loop(low, high, fill, 0)

        query = q_ref[at, :]
        halves = [pick_lanes(query, half) for half in range(2)]
        start = jnp.full((TILE, 128), -3e38, F32)

        def first(block, tops):
            cols = pl.ds(pl.multiple_of(block * TILE, TILE), TILE)
            keys = k_ref[cols, :]
            shade = bias[at, cols]
            out = []
            for half in range(2):
                part = dot_nt(halves[half], keys) + shade
                scores[half, :, cols] = part
                out.append(jnp.maximum(tops[half], jnp.maximum(part[:, :128], part[:, 128:])))
            return tuple(out)

        tops = lax.fori_loop(low, high, first, (start, start))
        tops = [jnp.max(top, axis=1, keepdims=True) for top in tops]

        def second(block, carry):
            cols = pl.ds(pl.multiple_of(block * TILE, TILE), TILE)
            values = v_ref[cols, :]
            out = []
            for half in range(2):
                total, acc = carry[2 * half], carry[2 * half + 1]
                probs = jnp.exp(scores[half, :, cols] - tops[half])
                total = total + (probs[:, :128] + probs[:, 128:])
                acc = acc + dot_nn(probs.astype(BF16), values)
                out += [total, acc]
            return tuple(out)

        zero = jnp.zeros((TILE, 128), F32)
        parts = lax.fori_loop(low, high, second, (zero,) * 4)
        done = []
        for half in range(2):
            total = jnp.sum(parts[2 * half], axis=1, keepdims=True)
            done.append(parts[2 * half + 1] / total)
            column = tops[half] + jnp.log(total)
            flat = jnp.transpose(jnp.broadcast_to(column, (TILE, 128)))
            lse_ref[0, half : half + 1, at] = flat[0:1, :]
        lanes = lax.broadcasted_iota(jnp.int32, (TILE, PAIR), 1)
        ctx_ref[at, :] = jnp.where(lanes < HEAD, done[0], done[1]).astype(BF16)


def attend(q, kv, span, segq, segk, padk):
    rows, width = q.shape
    window = kv.shape[0]
    pairs = width // PAIR
    whole = lambda shape: pl.BlockSpec(shape, lambda p, s: (0,) * len(shape))
    return pl.pallas_call(
        attend_kernel,
        grid_spec=pltpu.PrefetchScalarGridSpec(
            num_scalar_prefetch=1,
            grid=(pairs,),
            in_specs=[
                pl.BlockSpec((rows, PAIR), lambda p, s: (0, p)),
                pl.BlockSpec((window, PAIR), lambda p, s: (0, p)),
                pl.BlockSpec((window, PAIR), lambda p, s: (0, pairs + p)),
                whole((rows, 1)),
                whole((1, window)),
                whole((1, window)),
            ],
            out_specs=[
                pl.BlockSpec((rows, PAIR), lambda p, s: (0, p)),
                pl.BlockSpec((1, 8, rows), lambda p, s: (p, 0, 0)),
            ],
            scratch_shapes=[
                pltpu.VMEM((rows, window), F32),
                pltpu.VMEM((2, TILE, window), F32),
            ],
        ),
        out_shape=[
            jax.ShapeDtypeStruct((rows, width), BF16),
            jax.ShapeDtypeStruct((pairs, 8, rows), F32),
        ],
        name="attend",
    )(span, q, kv, kv, segq, segk, padk)


def attend_back_kernel(
    span, q_ref, k_ref, v_ref, dc_ref, lse_ref, segq, segk, padk, dq_ref, dk_ref, dv_ref, bias, dk_acc, dv_acc, keep_p, keep_d
):
    pair = pl.program_id(0)
    rows = q_ref.shape[0]
    window = k_ref.shape[0]
    tiles = rows // TILE
    dk_acc[...] = jnp.zeros_like(dk_acc)
    dv_acc[...] = jnp.zeros_like(dv_acc)
    for tile in range(tiles):
        at = slice(tile * TILE, (tile + 1) * TILE)
        low, high = span[tile, 0], span[tile, 1]

        @pl.when(pair == 0)
        def _():
            def fill(block, carry):
                keys = pl.ds(pl.multiple_of(block * TILE, TILE), TILE)
                key_at = lax.broadcasted_iota(jnp.int32, (TILE, TILE), 0) + block * TILE
                row_at = lax.broadcasted_iota(jnp.int32, (TILE, TILE), 1) + (REACH * TILE + tile * TILE)
                same = segk[keys, :] == segq[:, at]
                open_key = (padk[keys, :] == 1) | (row_at == key_at)
                bias[keys, at] = jnp.where(same & open_key, 0.0, -1e30)
                return carry
            lax.fori_loop(low, high, fill, 0)

        query = q_ref[at, :]
        dctx = dc_ref[at, :]
        q_half = [pick_lanes(query, half) for half in range(2)]
        c_half = [pick_lanes(dctx, half) for half in range(2)]

        zero = jnp.zeros((8, TILE), F32)

        def first(block, inner):
            keys = pl.ds(pl.multiple_of(block * TILE, TILE), TILE)
            key = k_ref[keys, :]
            value = v_ref[keys, :]
            shade = bias[keys, at]
            add_v = jnp.zeros((TILE, PAIR), F32)
            out = []
            for half in range(2):
                part = dot_nt(key, q_half[half]) + shade
                probs = jnp.exp(part - lse_ref[0, half : half + 1, at])
                dprobs = dot_nt(value, c_half[half])
                add_v = add_v + dot_nn(probs.astype(BF16), c_half[half])
                keep_p[half, keys, :] = probs
                keep_d[half, keys, :] = dprobs
                out.append(inner[half] + jnp.sum((probs * dprobs).reshape(TILE // 8, 8, TILE), axis=0))
            dv_acc[keys, :] += add_v
            return tuple(out)

        inner = lax.fori_loop(low, high, first, (zero, zero))
        inner = [jnp.sum(item, axis=0, keepdims=True) for item in inner]

        def second(block, dq):
            keys = pl.ds(pl.multiple_of(block * TILE, TILE), TILE)
            key = k_ref[keys, :]
            add_k = jnp.zeros((TILE, PAIR), F32)
            for half in range(2):
                dscore = (keep_p[half, keys, :] * (keep_d[half, keys, :] - inner[half])).astype(BF16)
                add_k = add_k + dot_nn(dscore, q_half[half])
                dq = dq + dot_tn(dscore, pick_lanes(key, half))
            dk_acc[keys, :] += add_k
            return dq

        dq = lax.fori_loop(low, high, second, jnp.zeros((TILE, PAIR), F32))
        dq_ref[at, :] = (dq * 0.125).astype(BF16)
    dk_ref[...] = dk_acc[...].astype(BF16)
    dv_ref[...] = dv_acc[...].astype(BF16)


def attend_back(q, kv, dctx, lse, span, segq, segk, padk):
    rows, width = q.shape
    window = kv.shape[0]
    pairs = width // PAIR
    whole = lambda shape: pl.BlockSpec(shape, lambda p, s: (0,) * len(shape))
    return pl.pallas_call(
        attend_back_kernel,
        grid_spec=pltpu.PrefetchScalarGridSpec(
            num_scalar_prefetch=1,
            grid=(pairs,),
            in_specs=[
                pl.BlockSpec((rows, PAIR), lambda p, s: (0, p)),
                pl.BlockSpec((window, PAIR), lambda p, s: (0, p)),
                pl.BlockSpec((window, PAIR), lambda p, s: (0, pairs + p)),
                pl.BlockSpec((rows, PAIR), lambda p, s: (0, p)),
                pl.BlockSpec((1, 8, rows), lambda p, s: (p, 0, 0)),
                whole((1, rows)),
                whole((window, 1)),
                whole((window, 1)),
            ],
            out_specs=[
                pl.BlockSpec((rows, PAIR), lambda p, s: (0, p)),
                pl.BlockSpec((window, PAIR), lambda p, s: (0, p)),
                pl.BlockSpec((window, PAIR), lambda p, s: (0, p)),
            ],
            scratch_shapes=[
                pltpu.VMEM((window, rows), F32),
                pltpu.VMEM((window, PAIR), F32),
                pltpu.VMEM((window, PAIR), F32),
                pltpu.VMEM((2, window, TILE), F32),
                pltpu.VMEM((2, window, TILE), F32),
            ],
        ),
        out_shape=[
            jax.ShapeDtypeStruct((rows, width), BF16),
            jax.ShapeDtypeStruct((window, width), BF16),
            jax.ShapeDtypeStruct((window, width), BF16),
        ],
        name="attend_back",
    )(span, q, kv, kv, dctx, lse, segq, segk, padk)


def norm_stats(resid):
    center = resid - jnp.mean(resid, axis=-1, keepdims=True)
    spread = jnp.mean(center * center, axis=-1, keepdims=True)
    scale = lax.rsqrt(spread + 1e-12)
    return center * scale, scale


def norm_back(grad, resid, gain):
    unit, scale = norm_stats(resid)
    inner = grad * gain
    back = scale * (
        inner - jnp.mean(inner, axis=-1, keepdims=True) - unit * jnp.mean(inner * unit, axis=-1, keepdims=True)
    )
    return back, jnp.sum(grad * unit, axis=0), jnp.sum(grad, axis=0)


class Place:
    def __init__(self):
        self.size = lax.axis_size("seq")
        self.seq = lax.axis_index("seq")
        self.core = lax.axis_index("dp")

    def flat(self, core, seq):
        return core * self.size + seq

    def move(self, block, delta):
        pairs = []
        for seq in range(self.size):
            for core in range(2):
                unit = 2 * (seq // LINE) + core + delta
                if 0 <= unit < 2 * (self.size // LINE):
                    pairs.append((self.flat(core, seq), self.flat(unit % 2, (unit // 2) * LINE + seq % LINE)))
        return lax.ppermute(block, ("dp", "seq"), pairs)

    def route(self, turn, back=False):
        pairs = []
        for seq in range(self.size):
            for core in range(2):
                spot = seq % LINE
                row = turn if seq % 2 == 0 else 1 - turn
                goal = self.flat(spot // 2, (seq // LINE) * LINE + 2 * core + row)
                pairs.append((self.flat(core, seq), goal))
        return [(b, a) for a, b in pairs] if back else pairs

    def take_in(self, both):
        even = self.seq % 2 == 0
        send = [jnp.where(even, both[t], both[1 - t]) for t in range(2)]
        got = [lax.ppermute(send[t], ("dp", "seq"), self.route(t)) for t in range(2)]
        odd_line = self.seq % 2 == 1
        first = jnp.where(odd_line, got[1], got[0])
        last = jnp.where(odd_line, got[0], got[1])
        return jnp.concatenate([first, last], axis=0)

    def give_back(self, own):
        half = own.shape[0] // 2
        first, last = own[:half], own[half:]
        odd_line = self.seq % 2 == 1
        send = [jnp.where(odd_line, last, first), jnp.where(odd_line, first, last)]
        got = [lax.ppermute(send[t], ("dp", "seq"), self.route(t, True)) for t in range(2)]
        even = self.seq % 2 == 0
        return jnp.stack([jnp.where(even, got[0], got[1]), jnp.where(even, got[1], got[0])])

    def widen(self, own):
        half = own.shape[0] // 2
        return jnp.concatenate(
            [self.move(own[half:], 2), self.move(own, 1), own, self.move(own, -1), self.move(own[:half], -2)], axis=0
        )

    def narrow(self, wide):
        half = wide.shape[0] // 8
        own = wide[3 * half : 5 * half]
        low = wide.astype(BF16)
        own = own + self.move(low[half : 3 * half], -1).astype(F32) + self.move(low[5 * half : 7 * half], 1).astype(F32)
        top = self.move(low[7 * half :], 2).astype(F32)
        bottom = self.move(low[:half], -2).astype(F32)
        return own + jnp.concatenate([top, bottom], axis=0)


def forward_layer(wide, state, full, marks):
    rows = state.shape[0]
    width = state.shape[1]
    w_qkv, b_q, b_v, w_out, b_out, gain1, shift1, w_up, b_up, w_down, b_down, gain2, shift2 = full
    span, segq, segk, padk = marks
    own = state.astype(BF16)
    q = ((dot_nn(own, w_qkv[:, :width]) + b_q) * 0.125).astype(BF16)
    bias = jnp.concatenate([jnp.zeros_like(b_v), b_v])
    kv = (dot_nn(wide, w_qkv[:, width:]) + bias).astype(BF16)
    ctx, lse = attend(q, kv, span, segq[:, None], segk[None], padk[None])
    resid1 = state + dot_nn(ctx, w_out) + b_out
    unit, _ = norm_stats(resid1)
    hidden = unit * gain1 + shift1
    hidden_low = hidden.astype(BF16)
    up = dot_nn(hidden_low, w_up) + b_up
    active = (up * (0.5 * (1.0 + lax.erf(up * (2.0**-0.5))))).astype(BF16)
    resid2 = hidden + dot_nn(active, w_down) + b_down
    unit, _ = norm_stats(resid2)
    result = unit * gain2 + shift2
    return result, (own, wide, q, kv, ctx, lse, resid1, hidden_low, up, active, resid2)


def backward_layer(grad, full, saved, marks):
    w_qkv, b_q, b_v, w_out, b_out, gain1, shift1, w_up, b_up, w_down, b_down, gain2, shift2 = full
    span, segq, segk, padk = marks
    own, wide, q, kv, ctx, lse, resid1, hidden_low, up, active, resid2 = saved
    rows, width = resid1.shape
    grad2, g_gain2, g_shift2 = norm_back(grad, resid2, gain2)
    d_ffn = grad2.astype(BF16)
    g_bdown = jnp.sum(d_ffn.astype(F32), axis=0)
    g_wdown = dot_tn(active, d_ffn)
    d_active = dot_nt(d_ffn, w_down)
    slope = 0.5 * (1.0 + lax.erf(up * (2.0**-0.5))) + up * jnp.exp(-0.5 * up * up) * 0.3989422804014327
    d_up = (d_active * slope).astype(BF16)
    g_wup = dot_tn(hidden_low, d_up)
    g_bup = jnp.sum(d_up.astype(F32), axis=0)
    d_hidden = grad2 + dot_nt(d_up, w_up)
    grad1, g_gain1, g_shift1 = norm_back(d_hidden, resid1, gain1)
    d_attn = grad1.astype(BF16)
    g_wout = dot_tn(ctx, d_attn)
    g_bout = jnp.sum(d_attn.astype(F32), axis=0)
    d_ctx = dot_nt(d_attn, w_out).astype(BF16)
    d_q, d_k, d_v = attend_back(q, kv, d_ctx, lse, span, segq[None], segk[:, None], padk[:, None])
    g_wq = dot_tn(own, d_q)
    g_wk = dot_tn(wide, d_k)
    g_wv = dot_tn(wide, d_v)
    g_wqkv = jnp.concatenate([g_wq, g_wk, g_wv], axis=1)
    g_bq = jnp.sum(d_q.astype(F32), axis=0)
    g_bv = jnp.sum(d_v.astype(F32), axis=0)
    d_wide = dot_nt(d_k, w_qkv[:, width : 2 * width]) + dot_nt(d_v, w_qkv[:, 2 * width :])
    d_own = grad1 + dot_nt(d_q, w_qkv[:, :width])
    grads = (
        g_wqkv, g_bq, g_bv, g_wout, g_bout, g_gain1, g_shift1, g_wup, g_bup, g_wdown, g_bdown, g_gain2, g_shift2
    )
    return d_wide, d_own, grads


def per_device(
    hidden_in, cotangent, segments, pad_mask, w_qkv, b_query, b_value, w_out, b_out, norm1_gain, norm1_bias,
    w_up, b_up, w_down, b_down, norm2_gain, norm2_bias,
):
    shards = (
        w_qkv, b_query, b_value, w_out, b_out, norm1_gain, norm1_bias, w_up, b_up, w_down, b_down, norm2_gain, norm2_bias
    )
    place = Place()
    both, half, width = hidden_in.shape
    rows = 2 * half
    window = 8 * half
    full = tuple(lax.all_gather(shard, ("dp", "seq"), axis=0, tiled=True) for shard in shards)
    full = tuple(item if item.ndim == 2 else item.astype(F32) for item in full)
    spot = place.seq % LINE
    tags = jnp.stack([segments, pad_mask])
    other = lax.ppermute(tags, "dp", [(0, 1), (1, 0)])
    tags = jnp.where(place.core == spot // 2, tags, other)
    tags = jnp.where(spot % 2 == 0, tags[:, 0], tags[:, 1])
    offset = (2 * (place.seq // LINE) + place.core) * rows
    margin = REACH * half
    seg_all = jnp.pad(jnp.pad(tags[0], (margin, 0), constant_values=-1), (0, margin), constant_values=1 << 30)
    pad_all = jnp.pad(tags[1], (margin, margin))
    segk = lax.dynamic_slice_in_dim(seg_all, offset, window)
    padk = lax.dynamic_slice_in_dim(pad_all, offset, window)
    segq = segk[margin : margin + rows]
    padq = padk[margin : margin + rows]
    spans = []
    for tile in range(rows // TILE):
        first, last = segq[tile * TILE], segq[(tile + 1) * TILE - 1]
        low = jnp.sum((segk < first).astype(jnp.int32))
        high = jnp.sum((segk <= last).astype(jnp.int32))
        spans.append(jnp.stack([low // TILE, (high + TILE - 1) // TILE]))
    span = jnp.stack(spans)
    marks = (span, segq, segk, padk)
    own_in = place.take_in(hidden_in)
    own_ct = place.take_in(cotangent)
    state0 = own_in.astype(F32)
    state1, saved1 = forward_layer(place.widen(own_in), state0, full, marks)
    state2, saved2 = forward_layer(place.widen(state1.astype(BF16)), state1, full, marks)
    out = place.give_back(state2.astype(BF16))
    grad = own_ct.astype(F32) * padq[:, None].astype(F32)
    d_wide, d_own, grads2 = backward_layer(grad, full, saved2, marks)
    grad = d_own + place.narrow(d_wide)
    d_wide, d_own, grads1 = backward_layer(grad, full, saved1, marks)
    grad = d_own + place.narrow(d_wide)
    grad_in = place.give_back(grad.astype(BF16)).astype(F32)
    totals = jax.tree.map(lambda a, b: a + b, grads2, grads1)
    summed = tuple(lax.psum_scatter(item, ("dp", "seq"), scatter_dimension=0, tiled=True) for item in totals)
    return (out, grad_in) + summed


def solution(mesh):
    split = P(("dp", "seq"))
    mats = P(("dp", "seq"), None)
    tokens = P("dp", "seq", None)
    weights = (mats, split, split, mats, split, split, split, mats, split, mats, split, split, split)
    return jax.shard_map(
        per_device,
        mesh=mesh,
        in_specs=(tokens, tokens, P("dp", None), P("dp", None)) + weights,
        out_specs=(tokens, tokens) + weights,
        check_vma=False,
    )
```

```python
import functools

import jax
import jax.numpy as jnp
from jax import lax
from jax.experimental import pallas as pl
from jax.experimental.pallas import tpu as pltpu
from jax.sharding import PartitionSpec as P

HEADS = 12
HEAD = 64
PAIR = 2 * HEAD
REACH = 3
TILE = 256
LINE = 4

F32 = jnp.float32
BF16 = jnp.bfloat16


MESH = pl.DeviceIdType.MESH


class Spot:
    def __init__(self, size):
        self.count = size // LINE
        self.core = lax.axis_index("dp")
        seq = lax.axis_index("seq")
        self.g = seq // LINE
        self.c = seq % LINE
        self.x = self.c % 2
        self.y = self.c // 2

    def at(self, core, g, y, x):
        return {"dp": core, "seq": g * LINE + y * 2 + x}

    @property
    def partner(self):
        return self.at(1 - self.core, self.g, self.y, self.x)

    @property
    def across_x(self):
        return self.at(self.core, self.g, self.y, 1 - self.x)

    @property
    def across_y(self):
        return self.at(self.core, self.g, 1 - self.y, self.x)

    def along(self, step):
        return self.at(self.core, self.g + step, self.y, self.x)


def greet(spot):
    barrier = pltpu.get_barrier_semaphore()
    for device in (spot.partner, spot.across_x, spot.across_y):
        pl.semaphore_signal(barrier, inc=1, device_id=device, device_id_type=MESH)

    @pl.when(spot.g > 0)
    def _():
        pl.semaphore_signal(barrier, inc=1, device_id=spot.along(-1), device_id_type=MESH)

    @pl.when(spot.g < spot.count - 1)
    def _():
        pl.semaphore_signal(barrier, inc=1, device_id=spot.along(1), device_id_type=MESH)

    ends = (spot.g == 0).astype(jnp.int32) + (spot.g == spot.count - 1).astype(jnp.int32)
    pl.semaphore_wait(barrier, 5 - ends)


def gather_kernel(size, plan, *refs):
    arrays = 1 + max(item[0] for item in plan)
    shards, fulls = refs[:arrays], refs[arrays : 2 * arrays]
    own_sem, side_send, side_recv, line_send, line_recv = refs[2 * arrays :]
    spot = Spot(size)
    count = spot.count
    e, g, y, x = spot.core, spot.g, spot.y, spot.x
    every = pl.ds(0, 2)
    chunks = range(len(plan))

    def view(chunk, core, gs, ys, xs):
        array, low, wide, _ = plan[chunk]
        return fulls[array].at[core, gs, ys, xs, :, pl.ds(low, wide)]

    def own(chunk):
        array, low, wide, _ = plan[chunk]
        return shards[array].at[:, pl.ds(low, wide)]

    def outer(chunk):
        return plan[chunk][3][0] == "z"

    def near(far, way):
        return g + far if way else g - far

    def valid(far, way):
        return (g + far < count) if way else (g >= far)

    def line(chunk, far, way):
        gs = near(far, way)
        src = dst = view(chunk, e, gs, y, x) if outer(chunk) else view(chunk, e, gs, every, every)
        if far == 0 and outer(chunk):
            src = own(chunk)
        return pltpu.make_async_remote_copy(
            src_ref=src, dst_ref=dst, send_sem=line_send.at[chunk, way, far], recv_sem=line_recv.at[chunk, way, far],
            device_id=spot.along(1 - 2 * way), device_id_type=MESH,
        )

    def line_in(chunk, far, way):
        gs = near(far, way)
        block = view(chunk, e, gs, y, x) if outer(chunk) else view(chunk, e, gs, every, every)
        return pltpu.make_async_remote_copy(
            src_ref=block, dst_ref=block, send_sem=line_send.at[chunk, way, far - 1],
            recv_sem=line_recv.at[chunk, way, far - 1], device_id=spot.along(1 - 2 * way), device_id_type=MESH,
        )

    def onward(far, way):
        return valid(far, way) & ((g > 0) if way else (g < count - 1))

    def inward(far, way):
        return valid(far, way)

    def side(chunk, kind, far, way):
        gs = near(far, way)
        order = plan[chunk][3]
        slot = 2 * far + way - 1 if far else 0
        if kind == 2:
            src = dst = view(chunk, e, gs, every, every)
        else:
            later = order.index("xy"[kind]) > order.index("yx"[kind])
            ys = every if kind == 0 and later else y
            xs = every if kind == 1 and later else x
            src = dst = view(chunk, e, gs, ys, xs)
            if far == 0 and not later:
                src = own(chunk)
        device = (spot.across_x, spot.across_y, spot.partner)[kind]
        return pltpu.make_async_remote_copy(
            src_ref=src, dst_ref=dst, send_sem=side_send.at[chunk, kind, slot], recv_sem=side_recv.at[chunk, kind, slot],
            device_id=device, device_id_type=MESH,
        )

    def pieces(far):
        return [(far, way) for way in range(2)] if far else [(0, 0)]

    def guarded(cond, action):
        pl.when(cond)(action)

    sent = []

    def push(cond, make):
        sent.append((cond, make))
        guarded(cond, lambda: make().start())

    def pull(cond, make):
        guarded(cond, lambda: make().wait_recv())

    def push_line(chunk, far, way):
        push(onward(far, way), lambda: line(chunk, far, way))

    def push_side(chunk, kind, far, way):
        push(valid(far, way), lambda: side(chunk, kind, far, way))

    def pull_side(chunk, kind, far, way):
        pull(valid(far, way), lambda: side(chunk, kind, far, way))

    def first_kind(chunk):
        return 0 if plan[chunk][3].index("x") < plan[chunk][3].index("y") else 1

    greet(spot)
    keeps = []
    for chunk in chunks:
        kind = first_kind(chunk)
        if outer(chunk):
            push_line(chunk, 0, 0)
            push_line(chunk, 0, 1)
        push_side(chunk, kind, 0, 0)
        keep = pltpu.make_async_copy(own(chunk), view(chunk, e, g, y, x), own_sem.at[chunk])
        keep.start()
        keeps.append(keep)
    for chunk in chunks:
        keeps[chunk].wait()
    for far in range(count):
        for chunk in chunks:
            kind = first_kind(chunk)
            for item in pieces(far):
                if outer(chunk):
                    if far:
                        pull(inward(*item), lambda: line_in(chunk, *item))
                        if far < count - 1:
                            push_line(chunk, *item)
                        push_side(chunk, kind, *item)
                elif far:
                    pull(inward(*item), lambda: line_in(chunk, *item))
                    if far < count - 1:
                        push_line(chunk, *item)
                    push_side(chunk, 2, *item)
        for chunk in chunks:
            kind = first_kind(chunk)
            for item in pieces(far):
                if outer(chunk) or far == 0:
                    pull_side(chunk, kind, *item)
                    push_side(chunk, 1 - kind, *item)
        for chunk in chunks:
            kind = first_kind(chunk)
            for item in pieces(far):
                if outer(chunk) or far == 0:
                    pull_side(chunk, 1 - kind, *item)
                    if not outer(chunk):
                        push_line(chunk, 0, 0)
                        push_line(chunk, 0, 1)
                    push_side(chunk, 2, *item)
    for far in range(count):
        for chunk in chunks:
            for item in pieces(far):
                pull_side(chunk, 2, *item)
    for cond, make in sent:
        guarded(cond, lambda: make().wait_send())


def gather_all(shards, plan, size, ident):
    count = size // LINE
    chunks = len(plan)
    outs = [jax.ShapeDtypeStruct((2, count, 2, 2) + item.shape, item.dtype) for item in shards]
    hops = max(count - 1, 1)
    dma = pltpu.SemaphoreType.DMA
    return pl.pallas_call(
        functools.partial(gather_kernel, size, plan),
        out_shape=outs,
        in_specs=[pl.BlockSpec(memory_space=pltpu.VMEM)] * len(shards),
        out_specs=[pl.BlockSpec(memory_space=pl.ANY)] * len(shards),
        scratch_shapes=[dma((chunks,)), dma((chunks, 3, 2 * count - 1)), dma((chunks, 3, 2 * count - 1)), dma((chunks, 2, hops)), dma((chunks, 2, hops))],
        compiler_params=pltpu.CompilerParams(collective_id=ident, has_side_effects=True),
        name="gather_all",
    )(*shards)


def scatter_kernel(size, plan, arrays, *refs):
    grads, outs = refs[:arrays], refs[arrays : 2 * arrays]
    chunks = range(len(plan))
    held = refs[2 * arrays : 3 * arrays]
    from_side = refs[3 * arrays : 3 * arrays + len(plan)]
    from_last = refs[3 * arrays + len(plan) : 3 * arrays + 2 * len(plan)]
    from_line = refs[3 * arrays + 2 * len(plan) : 3 * arrays + 3 * len(plan)]
    side_send, side_recv, line_send, line_recv = refs[3 * arrays + 3 * len(plan) :]
    spot = Spot(size)
    count = spot.count
    e, g, y, x = spot.core, spot.g, spot.y, spot.x
    every = pl.ds(0, 2)
    sent = []

    def near(far, way):
        return g + far if way else g - far

    def valid(far, way):
        return (g + far < count) if way else (g >= far)

    def cols(chunk):
        return pl.ds(plan[chunk][1], plan[chunk][2])

    def part(chunk, gs, ys, xs):
        return held[plan[chunk][0]].at[gs, ys, xs, :, cols(chunk)]

    def slot(far, way):
        return 2 * far + way - 1 if far else 0

    def side(chunk, kind, far, way):
        gs = near(far, way)
        array, _, _, first = plan[chunk]
        if kind == 2:
            src = grads[array].at[1 - e, gs, :, :, :, cols(chunk)]
            dst = part(chunk, gs, every, every)
            device = spot.partner
        else:
            across = (spot.across_x, spot.across_y)[(0 if first == "x" else 1) ^ kind]
            device = across
            if kind == 0:
                src = part(chunk, gs, every, 1 - x) if first == "x" else part(chunk, gs, 1 - y, every)
                dst = from_side[chunk].at[gs]
            else:
                src = part(chunk, gs, 1 - y, x) if first == "x" else part(chunk, gs, y, 1 - x)
                dst = from_last[chunk].at[gs]
        return pltpu.make_async_remote_copy(
            src_ref=src, dst_ref=dst, send_sem=side_send.at[chunk, kind, slot(far, way)],
            recv_sem=side_recv.at[chunk, kind, slot(far, way)], device_id=device, device_id_type=MESH,
        )

    def line(chunk, far, way):
        gs = near(far, way)
        return pltpu.make_async_remote_copy(
            src_ref=part(chunk, gs, y, x), dst_ref=from_line[chunk].at[way, far - 1],
            send_sem=line_send.at[chunk, way, far - 1], recv_sem=line_recv.at[chunk, way, far - 1],
            device_id=spot.along(2 * way - 1), device_id_type=MESH,
        )

    def arrive(chunk, far, way):
        block = from_line[chunk].at[way, far]
        return pltpu.make_async_remote_copy(
            src_ref=block, dst_ref=block, send_sem=line_send.at[chunk, way, far], recv_sem=line_recv.at[chunk, way, far],
            device_id=spot.along(2 * way - 1), device_id_type=MESH,
        )

    def push(far, way, make):
        sent.append((far, way, make))
        make().start()

    def add_into(target, other):
        target[...] = (target[...].astype(F32) + other[...].astype(F32)).astype(target.dtype)

    def stage_one(chunk, far, way):
        gs = near(far, way)
        side(chunk, 2, far, way).wait_recv()
        array = plan[chunk][0]

        def body(index, carry):
            ys, xs = index // 2, index % 2
            add_into(part(chunk, gs, ys, xs), grads[array].at[e, gs, ys, xs, :, cols(chunk)])
            return carry

        lax.fori_loop(0, 4, body, 0)
        push(far, way, lambda: side(chunk, 0, far, way))

    def stage_two(chunk, far, way):
        gs = near(far, way)
        side(chunk, 0, far, way).wait_recv()

        def body(index, carry):
            mine = part(chunk, gs, index, x) if plan[chunk][3] == "x" else part(chunk, gs, y, index)
            add_into(mine, from_side[chunk].at[gs, index])
            return carry

        lax.fori_loop(0, 2, body, 0)
        push(far, way, lambda: side(chunk, 1, far, way))

    def stage_three(chunk, far, way):
        gs = near(far, way)
        side(chunk, 1, far, way).wait_recv()
        mine = part(chunk, gs, y, x)
        if far == 0:
            array, low, wide, _ = plan[chunk]
            out = outs[array].at[:, pl.ds(low, wide)]
            out[...] = mine[...].astype(F32) + from_last[chunk][gs].astype(F32)
            for side_way in range(2):
                @pl.when((g > 0) if side_way else (g < count - 1))
                def _():
                    arrive(chunk, 0, side_way).wait_recv()
                    out[...] += from_line[chunk][side_way, 0].astype(F32)
        else:
            add_into(mine, from_last[chunk].at[gs])
            @pl.when((g > 0) if way else (g < count - 1))
            def _():
                if far < count - 1:
                    arrive(chunk, far, way).wait_recv()
                    add_into(mine, from_line[chunk].at[way, far])
            push(far, way, lambda: line(chunk, far, way))

    greet(spot)
    pieces = [(far, way) for far in range(count - 1, 0, -1) for way in range(2)] + [(0, 0)]

    def run(stage, chunk, far, way):
        pl.when(valid(far, way))(lambda: stage(chunk, far, way))

    for far, way in pieces:
        for chunk in chunks:
            run(lambda c, f, w: push(f, w, lambda: side(c, 2, f, w)), chunk, far, way)
    stages = (stage_one, stage_two, stage_three)
    lag = (0, 2, 4)
    for step in range(len(pieces) + lag[-1]):
        for stage, delay in zip(stages, lag):
            if 0 <= step - delay < len(pieces):
                for chunk in chunks:
                    run(stage, chunk, *pieces[step - delay])
    for far, way, make in sent:
        pl.when(valid(far, way))(lambda: make().wait_send())


def scatter_all(grads, plan, size, ident):
    count = size // LINE
    chunks = len(plan)
    shapes = [item.shape[-2:] for item in grads]
    dma = pltpu.SemaphoreType.DMA
    hops = max(count - 1, 1)
    vmem = pltpu.VMEM
    scratch = [vmem((count, 2, 2) + shape, item.dtype) for shape, item in zip(shapes, grads)]
    for lead in ((count, 2), (count,), (2, hops)):
        scratch += [vmem(lead + (shapes[array][0], wide), grads[array].dtype) for array, _, wide, _ in plan]
    scratch += [dma((chunks, 3, 2 * count - 1))] * 2 + [dma((chunks, 2, hops))] * 2
    return pl.pallas_call(
        functools.partial(scatter_kernel, size, plan, len(grads)),
        out_shape=[jax.ShapeDtypeStruct(shape, F32) for shape in shapes],
        in_specs=[pl.BlockSpec(memory_space=pltpu.VMEM)] * len(grads),
        out_specs=[pl.BlockSpec(memory_space=pltpu.VMEM)] * len(grads),
        scratch_shapes=scratch,
        compiler_params=pltpu.CompilerParams(collective_id=ident, has_side_effects=True, vmem_limit_bytes=62 << 20),
        name="scatter_all",
    )(*grads)


def pick_lanes(block, half):
    lanes = lax.broadcasted_iota(jnp.int32, block.shape, 1)
    keep = (lanes < HEAD) if half == 0 else (lanes >= HEAD)
    return jnp.where(keep, block, jnp.zeros_like(block))


def dot_nt(left, right):
    return lax.dot_general(left, right, (((1,), (1,)), ((), ())), preferred_element_type=F32)


def dot_tn(left, right):
    return lax.dot_general(left, right, (((0,), (0,)), ((), ())), preferred_element_type=F32)


def dot_nn(left, right):
    return lax.dot_general(left, right, (((1,), (0,)), ((), ())), preferred_element_type=F32)


def attend_kernel(span, q_ref, k_ref, v_ref, segq, segk, padk, ctx_ref, lse_ref, bias, scores):
    pair = pl.program_id(0)
    rows = q_ref.shape[0]
    window = k_ref.shape[0]
    tiles = rows // TILE
    for tile in range(tiles):
        at = slice(tile * TILE, (tile + 1) * TILE)
        low, high = span[tile, 0], span[tile, 1]

        @pl.when(pair == 0)
        def _():
            def fill(block, carry):
                cols = pl.ds(pl.multiple_of(block * TILE, TILE), TILE)
                row_at = lax.broadcasted_iota(jnp.int32, (TILE, TILE), 0) + (REACH * TILE + tile * TILE)
                col_at = lax.broadcasted_iota(jnp.int32, (TILE, TILE), 1) + block * TILE
                same = segq[at, :] == segk[:, cols]
                open_key = (padk[:, cols] == 1) | (row_at == col_at)
                bias[at, cols] = jnp.where(same & open_key, 0.0, -1e30)
                return carry
            lax.fori_loop(low, high, fill, 0)

        query = q_ref[at, :]
        halves = [pick_lanes(query, half) for half in range(2)]
        start = jnp.full((TILE, 128), -3e38, F32)

        def first(block, tops):
            cols = pl.ds(pl.multiple_of(block * TILE, TILE), TILE)
            keys = k_ref[cols, :]
            shade = bias[at, cols]
            out = []
            for half in range(2):
                part = dot_nt(halves[half], keys) + shade
                scores[half, :, cols] = part
                out.append(jnp.maximum(tops[half], jnp.maximum(part[:, :128], part[:, 128:])))
            return tuple(out)

        tops = lax.fori_loop(low, high, first, (start, start))
        tops = [jnp.max(top, axis=1, keepdims=True) for top in tops]

        def second(block, carry):
            cols = pl.ds(pl.multiple_of(block * TILE, TILE), TILE)
            values = v_ref[cols, :]
            out = []
            for half in range(2):
                total, acc = carry[2 * half], carry[2 * half + 1]
                probs = jnp.exp(scores[half, :, cols] - tops[half])
                total = total + (probs[:, :128] + probs[:, 128:])
                acc = acc + dot_nn(probs.astype(BF16), values)
                out += [total, acc]
            return tuple(out)

        zero = jnp.zeros((TILE, 128), F32)
        parts = lax.fori_loop(low, high, second, (zero,) * 4)
        done = []
        for half in range(2):
            total = jnp.sum(parts[2 * half], axis=1, keepdims=True)
            done.append(parts[2 * half + 1] / total)
            column = tops[half] + jnp.log(total)
            flat = jnp.transpose(jnp.broadcast_to(column, (TILE, 128)))
            lse_ref[0, half : half + 1, at] = flat[0:1, :]
        lanes = lax.broadcasted_iota(jnp.int32, (TILE, PAIR), 1)
        ctx_ref[at, :] = jnp.where(lanes < HEAD, done[0], done[1]).astype(BF16)


def attend(q, kv, span, segq, segk, padk):
    rows, width = q.shape
    window = kv.shape[0]
    pairs = width // PAIR
    whole = lambda shape: pl.BlockSpec(shape, lambda p, s: (0,) * len(shape))
    return pl.pallas_call(
        attend_kernel,
        grid_spec=pltpu.PrefetchScalarGridSpec(
            num_scalar_prefetch=1,
            grid=(pairs,),
            in_specs=[
                pl.BlockSpec((rows, PAIR), lambda p, s: (0, p)),
                pl.BlockSpec((window, PAIR), lambda p, s: (0, p)),
                pl.BlockSpec((window, PAIR), lambda p, s: (0, pairs + p)),
                whole((rows, 1)),
                whole((1, window)),
                whole((1, window)),
            ],
            out_specs=[
                pl.BlockSpec((rows, PAIR), lambda p, s: (0, p)),
                pl.BlockSpec((1, 8, rows), lambda p, s: (p, 0, 0)),
            ],
            scratch_shapes=[
                pltpu.VMEM((rows, window), F32),
                pltpu.VMEM((2, TILE, window), F32),
            ],
        ),
        out_shape=[
            jax.ShapeDtypeStruct((rows, width), BF16),
            jax.ShapeDtypeStruct((pairs, 8, rows), F32),
        ],
        name="attend",
    )(span, q, kv, kv, segq, segk, padk)


def attend_back_kernel(
    span, q_ref, k_ref, v_ref, dc_ref, lse_ref, segq, segk, padk, dq_ref, dk_ref, dv_ref, bias, dk_acc, dv_acc, keep_p, keep_d
):
    pair = pl.program_id(0)
    rows = q_ref.shape[0]
    window = k_ref.shape[0]
    tiles = rows // TILE
    dk_acc[...] = jnp.zeros_like(dk_acc)
    dv_acc[...] = jnp.zeros_like(dv_acc)
    for tile in range(tiles):
        at = slice(tile * TILE, (tile + 1) * TILE)
        low, high = span[tile, 0], span[tile, 1]

        @pl.when(pair == 0)
        def _():
            def fill(block, carry):
                keys = pl.ds(pl.multiple_of(block * TILE, TILE), TILE)
                key_at = lax.broadcasted_iota(jnp.int32, (TILE, TILE), 0) + block * TILE
                row_at = lax.broadcasted_iota(jnp.int32, (TILE, TILE), 1) + (REACH * TILE + tile * TILE)
                same = segk[keys, :] == segq[:, at]
                open_key = (padk[keys, :] == 1) | (row_at == key_at)
                bias[keys, at] = jnp.where(same & open_key, 0.0, -1e30)
                return carry
            lax.fori_loop(low, high, fill, 0)

        query = q_ref[at, :]
        dctx = dc_ref[at, :]
        q_half = [pick_lanes(query, half) for half in range(2)]
        c_half = [pick_lanes(dctx, half) for half in range(2)]

        zero = jnp.zeros((8, TILE), F32)

        def first(block, inner):
            keys = pl.ds(pl.multiple_of(block * TILE, TILE), TILE)
            key = k_ref[keys, :]
            value = v_ref[keys, :]
            shade = bias[keys, at]
            add_v = jnp.zeros((TILE, PAIR), F32)
            out = []
            for half in range(2):
                part = dot_nt(key, q_half[half]) + shade
                probs = jnp.exp(part - lse_ref[0, half : half + 1, at])
                dprobs = dot_nt(value, c_half[half])
                add_v = add_v + dot_nn(probs.astype(BF16), c_half[half])
                keep_p[half, keys, :] = probs
                keep_d[half, keys, :] = dprobs
                out.append(inner[half] + jnp.sum((probs * dprobs).reshape(TILE // 8, 8, TILE), axis=0))
            dv_acc[keys, :] += add_v
            return tuple(out)

        inner = lax.fori_loop(low, high, first, (zero, zero))
        inner = [jnp.sum(item, axis=0, keepdims=True) for item in inner]

        def second(block, dq):
            keys = pl.ds(pl.multiple_of(block * TILE, TILE), TILE)
            key = k_ref[keys, :]
            add_k = jnp.zeros((TILE, PAIR), F32)
            for half in range(2):
                dscore = (keep_p[half, keys, :] * (keep_d[half, keys, :] - inner[half])).astype(BF16)
                add_k = add_k + dot_nn(dscore, q_half[half])
                dq = dq + dot_tn(dscore, pick_lanes(key, half))
            dk_acc[keys, :] += add_k
            return dq

        dq = lax.fori_loop(low, high, second, jnp.zeros((TILE, PAIR), F32))
        dq_ref[at, :] = (dq * 0.125).astype(BF16)
    dk_ref[...] = dk_acc[...].astype(BF16)
    dv_ref[...] = dv_acc[...].astype(BF16)


def attend_back(q, kv, dctx, lse, span, segq, segk, padk):
    rows, width = q.shape
    window = kv.shape[0]
    pairs = width // PAIR
    whole = lambda shape: pl.BlockSpec(shape, lambda p, s: (0,) * len(shape))
    return pl.pallas_call(
        attend_back_kernel,
        grid_spec=pltpu.PrefetchScalarGridSpec(
            num_scalar_prefetch=1,
            grid=(pairs,),
            in_specs=[
                pl.BlockSpec((rows, PAIR), lambda p, s: (0, p)),
                pl.BlockSpec((window, PAIR), lambda p, s: (0, p)),
                pl.BlockSpec((window, PAIR), lambda p, s: (0, pairs + p)),
                pl.BlockSpec((rows, PAIR), lambda p, s: (0, p)),
                pl.BlockSpec((1, 8, rows), lambda p, s: (p, 0, 0)),
                whole((1, rows)),
                whole((window, 1)),
                whole((window, 1)),
            ],
            out_specs=[
                pl.BlockSpec((rows, PAIR), lambda p, s: (0, p)),
                pl.BlockSpec((window, PAIR), lambda p, s: (0, p)),
                pl.BlockSpec((window, PAIR), lambda p, s: (0, p)),
            ],
            scratch_shapes=[
                pltpu.VMEM((window, rows), F32),
                pltpu.VMEM((window, PAIR), F32),
                pltpu.VMEM((window, PAIR), F32),
                pltpu.VMEM((2, window, TILE), F32),
                pltpu.VMEM((2, window, TILE), F32),
            ],
        ),
        out_shape=[
            jax.ShapeDtypeStruct((rows, width), BF16),
            jax.ShapeDtypeStruct((window, width), BF16),
            jax.ShapeDtypeStruct((window, width), BF16),
        ],
        name="attend_back",
    )(span, q, kv, kv, dctx, lse, segq, segk, padk)


def norm_stats(resid):
    center = resid - jnp.mean(resid, axis=-1, keepdims=True)
    spread = jnp.mean(center * center, axis=-1, keepdims=True)
    scale = lax.rsqrt(spread + 1e-12)
    return center * scale, scale


def norm_back(grad, resid, gain):
    unit, scale = norm_stats(resid)
    inner = grad * gain
    back = scale * (
        inner - jnp.mean(inner, axis=-1, keepdims=True) - unit * jnp.mean(inner * unit, axis=-1, keepdims=True)
    )
    return back, jnp.sum(grad * unit, axis=0), jnp.sum(grad, axis=0)


class Place:
    def __init__(self):
        self.size = lax.axis_size("seq")
        self.seq = lax.axis_index("seq")
        self.core = lax.axis_index("dp")

    def flat(self, core, seq):
        return core * self.size + seq

    def move(self, block, delta):
        pairs = []
        for seq in range(self.size):
            for core in range(2):
                unit = 2 * (seq // LINE) + core + delta
                if 0 <= unit < 2 * (self.size // LINE):
                    pairs.append((self.flat(core, seq), self.flat(unit % 2, (unit // 2) * LINE + seq % LINE)))
        return lax.ppermute(block, ("dp", "seq"), pairs)

    def route(self, turn, back=False):
        pairs = []
        for seq in range(self.size):
            for core in range(2):
                spot = seq % LINE
                row = turn if seq % 2 == 0 else 1 - turn
                goal = self.flat(spot // 2, (seq // LINE) * LINE + 2 * core + row)
                pairs.append((self.flat(core, seq), goal))
        return [(b, a) for a, b in pairs] if back else pairs

    def take_in(self, both):
        even = self.seq % 2 == 0
        send = [jnp.where(even, both[t], both[1 - t]) for t in range(2)]
        got = [lax.ppermute(send[t], ("dp", "seq"), self.route(t)) for t in range(2)]
        odd_line = self.seq % 2 == 1
        first = jnp.where(odd_line, got[1], got[0])
        last = jnp.where(odd_line, got[0], got[1])
        return jnp.concatenate([first, last], axis=0)

    def give_back(self, own):
        half = own.shape[0] // 2
        first, last = own[:half], own[half:]
        odd_line = self.seq % 2 == 1
        send = [jnp.where(odd_line, last, first), jnp.where(odd_line, first, last)]
        got = [lax.ppermute(send[t], ("dp", "seq"), self.route(t, True)) for t in range(2)]
        even = self.seq % 2 == 0
        return jnp.stack([jnp.where(even, got[0], got[1]), jnp.where(even, got[1], got[0])])

    def widen(self, own):
        half = own.shape[0] // 2
        return jnp.concatenate(
            [self.move(own[half:], 2), self.move(own, 1), own, self.move(own, -1), self.move(own[:half], -2)], axis=0
        )

    def narrow(self, wide):
        half = wide.shape[0] // 8
        own = wide[3 * half : 5 * half]
        low = wide.astype(BF16)
        own = own + self.move(low[half : 3 * half], -1).astype(F32) + self.move(low[5 * half : 7 * half], 1).astype(F32)
        top = self.move(low[7 * half :], 2).astype(F32)
        bottom = self.move(low[:half], -2).astype(F32)
        return own + jnp.concatenate([top, bottom], axis=0)


def forward_layer(wide, state, full, marks):
    rows = state.shape[0]
    width = state.shape[1]
    w_qkv, b_q, b_v, w_out, b_out, gain1, shift1, w_up, b_up, w_down, b_down, gain2, shift2 = full
    span, segq, segk, padk = marks
    own = state.astype(BF16)
    q = ((dot_nn(own, w_qkv[:, :width]) + b_q) * 0.125).astype(BF16)
    bias = jnp.concatenate([jnp.zeros_like(b_v), b_v])
    kv = (dot_nn(wide, w_qkv[:, width:]) + bias).astype(BF16)
    ctx, lse = attend(q, kv, span, segq[:, None], segk[None], padk[None])
    resid1 = state + dot_nn(ctx, w_out) + b_out
    unit, _ = norm_stats(resid1)
    hidden = unit * gain1 + shift1
    hidden_low = hidden.astype(BF16)
    up = dot_nn(hidden_low, w_up) + b_up
    active = (up * (0.5 * (1.0 + lax.erf(up * (2.0**-0.5))))).astype(BF16)
    resid2 = hidden + dot_nn(active, w_down) + b_down
    unit, _ = norm_stats(resid2)
    result = unit * gain2 + shift2
    return result, (own, wide, q, kv, ctx, lse, resid1, hidden_low, up, active, resid2)


def backward_layer(grad, full, saved, marks):
    w_qkv, b_q, b_v, w_out, b_out, gain1, shift1, w_up, b_up, w_down, b_down, gain2, shift2 = full
    span, segq, segk, padk = marks
    own, wide, q, kv, ctx, lse, resid1, hidden_low, up, active, resid2 = saved
    rows, width = resid1.shape
    grad2, g_gain2, g_shift2 = norm_back(grad, resid2, gain2)
    d_ffn = grad2.astype(BF16)
    g_bdown = jnp.sum(d_ffn.astype(F32), axis=0)
    g_wdown = dot_tn(active, d_ffn)
    d_active = dot_nt(d_ffn, w_down)
    slope = 0.5 * (1.0 + lax.erf(up * (2.0**-0.5))) + up * jnp.exp(-0.5 * up * up) * 0.3989422804014327
    d_up = (d_active * slope).astype(BF16)
    g_wup = dot_tn(hidden_low, d_up)
    g_bup = jnp.sum(d_up.astype(F32), axis=0)
    d_hidden = grad2 + dot_nt(d_up, w_up)
    grad1, g_gain1, g_shift1 = norm_back(d_hidden, resid1, gain1)
    d_attn = grad1.astype(BF16)
    g_wout = dot_tn(ctx, d_attn)
    g_bout = jnp.sum(d_attn.astype(F32), axis=0)
    d_ctx = dot_nt(d_attn, w_out).astype(BF16)
    d_q, d_k, d_v = attend_back(q, kv, d_ctx, lse, span, segq[None], segk[:, None], padk[:, None])
    g_wq = dot_tn(own, d_q)
    g_wk = dot_tn(wide, d_k)
    g_wv = dot_tn(wide, d_v)
    g_wqkv = jnp.concatenate([g_wq, g_wk, g_wv], axis=1)
    g_bq = jnp.sum(d_q.astype(F32), axis=0)
    g_bv = jnp.sum(d_v.astype(F32), axis=0)
    d_wide = dot_nt(d_k, w_qkv[:, width : 2 * width]) + dot_nt(d_v, w_qkv[:, 2 * width :])
    d_own = grad1 + dot_nt(d_q, w_qkv[:, :width])
    grads = (
        g_wqkv, g_bq, g_bv, g_wout, g_bout, g_gain1, g_shift1, g_wup, g_bup, g_wdown, g_bdown, g_gain2, g_shift2
    )
    return d_wide, d_own, grads


MATRICES = (0, 3, 7, 9)
VECTORS = (1, 2, 4, 5, 6, 8, 10, 11, 12)
SLAB = (8, 128)


def gather_plan(widths):
    qkv, out, up, down = widths
    third = qkv // 3
    return [
        (2, 0, up, "zyxp"), (3, 0, down, "zxyp"), (1, 0, out, "xyzp"), (4, 0, SLAB[1], "xyzp"),
        (0, 0, third, "zxyp"), (0, third, third, "zyxp"), (0, 2 * third, third, "xyzp"),
    ]


def scatter_plan(widths):
    qkv, out, up, down = widths
    third = qkv // 3
    return [
        (4, 0, SLAB[1], "x"), (2, 0, up, "x"), (3, 0, down, "y"), (1, 0, out, "x"),
        (0, 0, third, "x"), (0, third, qkv - third, "y"),
    ]


def gather_weights(shards, size):
    mats = [shards[k] for k in MATRICES]
    flat = jnp.concatenate([shards[k] for k in VECTORS])
    slab = jnp.pad(flat, (0, SLAB[0] * SLAB[1] - flat.shape[0])).reshape(SLAB)
    got = gather_all(mats + [slab], gather_plan([item.shape[1] for item in mats]), size, 0)
    full = [None] * len(shards)
    for k, item in zip(MATRICES, got):
        full[k] = item.reshape(-1, item.shape[-1])
    rows = got[-1].reshape(2 * size, -1).astype(F32)
    low = 0
    for k in VECTORS:
        wide = shards[k].shape[0]
        full[k] = rows[:, low : low + wide].reshape(-1)
        low += wide
    return tuple(full)


def scatter_grads(totals, shards, size):
    lead = (2, size // LINE, 2, 2)
    mats = [totals[k].astype(BF16).reshape(lead + shards[k].shape) for k in MATRICES]
    flat = jnp.concatenate([totals[k].reshape(2 * size, -1) for k in VECTORS], axis=1)
    slab = jnp.pad(flat, ((0, 0), (0, SLAB[0] * SLAB[1] - flat.shape[1]))).reshape(lead + SLAB)
    got = scatter_all(mats + [slab], scatter_plan([item.shape[-1] for item in mats]), size, 1)
    summed = [None] * len(shards)
    for k, item in zip(MATRICES, got):
        summed[k] = item
    row = got[-1].reshape(-1)
    low = 0
    for k in VECTORS:
        wide = shards[k].shape[0]
        summed[k] = row[low : low + wide]
        low += wide
    return tuple(summed)


def per_device(
    hidden_in, cotangent, segments, pad_mask, w_qkv, b_query, b_value, w_out, b_out, norm1_gain, norm1_bias,
    w_up, b_up, w_down, b_down, norm2_gain, norm2_bias,
):
    shards = (
        w_qkv, b_query, b_value, w_out, b_out, norm1_gain, norm1_bias, w_up, b_up, w_down, b_down, norm2_gain, norm2_bias
    )
    place = Place()
    both, half, width = hidden_in.shape
    rows = 2 * half
    window = 8 * half
    full = gather_weights(shards, place.size)
    spot = place.seq % LINE
    tags = jnp.stack([segments, pad_mask])
    other = lax.ppermute(tags, "dp", [(0, 1), (1, 0)])
    tags = jnp.where(place.core == spot // 2, tags, other)
    tags = jnp.where(spot % 2 == 0, tags[:, 0], tags[:, 1])
    offset = (2 * (place.seq // LINE) + place.core) * rows
    margin = REACH * half
    seg_all = jnp.pad(jnp.pad(tags[0], (margin, 0), constant_values=-1), (0, margin), constant_values=1 << 30)
    pad_all = jnp.pad(tags[1], (margin, margin))
    segk = lax.dynamic_slice_in_dim(seg_all, offset, window)
    padk = lax.dynamic_slice_in_dim(pad_all, offset, window)
    segq = segk[margin : margin + rows]
    padq = padk[margin : margin + rows]
    spans = []
    for tile in range(rows // TILE):
        first, last = segq[tile * TILE], segq[(tile + 1) * TILE - 1]
        low = jnp.sum((segk < first).astype(jnp.int32))
        high = jnp.sum((segk <= last).astype(jnp.int32))
        spans.append(jnp.stack([low // TILE, (high + TILE - 1) // TILE]))
    span = jnp.stack(spans)
    marks = (span, segq, segk, padk)
    own_in = place.take_in(hidden_in)
    own_ct = place.take_in(cotangent)
    state0 = own_in.astype(F32)
    state1, saved1 = forward_layer(place.widen(own_in), state0, full, marks)
    state2, saved2 = forward_layer(place.widen(state1.astype(BF16)), state1, full, marks)
    out = place.give_back(state2.astype(BF16))
    grad = own_ct.astype(F32) * padq[:, None].astype(F32)
    d_wide, d_own, grads2 = backward_layer(grad, full, saved2, marks)
    grad = d_own + place.narrow(d_wide)
    d_wide, d_own, grads1 = backward_layer(grad, full, saved1, marks)
    grad = d_own + place.narrow(d_wide)
    grad_in = place.give_back(grad.astype(BF16)).astype(F32)
    totals = jax.tree.map(lambda a, b: a + b, grads2, grads1)
    summed = scatter_grads(totals, shards, place.size)
    return (out, grad_in) + summed


def solution(mesh):
    split = P(("dp", "seq"))
    mats = P(("dp", "seq"), None)
    tokens = P("dp", "seq", None)
    weights = (mats, split, split, mats, split, split, split, mats, split, mats, split, split, split)
    return jax.shard_map(
        per_device,
        mesh=mesh,
        in_specs=(tokens, tokens, P("dp", None), P("dp", None)) + weights,
        out_specs=(tokens, tokens) + weights,
        check_vma=False,
    )
```
